32 devices in a mesh: tensor: 4 (over z), dp: 2 (over y), section: 4 (over x, core).
Axes of the slice: x: 2, y: 2, z: 4, core: 2. Of those that a mesh axis runs over, the one named last changes fastest.
Arguments:
- basis_grad: bfloat16 [14336, 14336], P(('dp', 'section'), 'tensor'), may hold values from -0.046875 to 0.046875
- query: bfloat16 [14336, 4096], P('tensor', ('dp', 'section')), may hold values from -6 to 6
- basis_act: bfloat16 [4096, 4096], P(('dp', 'section'), 'tensor'), may hold values from -0.09375 to 0.09375
- eig_vals: float32 [14336, 4096], P(('dp', 'section'), 'tensor'), may hold values from 0.05 to 5
- grad_out: bfloat16 [512, 14336], P('section', 'tensor'), may hold values from -0.046875 to 0.046875
- act_in: bfloat16 [512, 4096], P('section', 'tensor'), may hold values from -0.09375 to 0.09375
Outputs:
- precond: bfloat16 [14336, 4096], P(('dp', 'section'), 'tensor')
- scores: float32 [512], P('tensor')
The draws below stay inside these ranges and needn't reach their ends.
All inputs are finite; a program needn't handle non-finite values.
Results may differ from the reference program's by a relative error of at most 0.015.
Values may be sent and summed in bfloat16 or wider, within the bound.
No kernel may reach another device: no remote copies, remote signals or barrier semaphores. Data moves between devices by JAX's collectives and lax.ppermute only.
A program may use at most 128 MiB of HBM per device.

```python
import math
import jax
import jax.numpy as jnp
from jax import lax

FF = 14336
D = 4096
TOKENS = 512
N_TENSOR = 4


def level_of(own_key, extent, pieces, least, largest):
    def one(position, parts):
        steps = jax.random.uniform(jax.random.fold_in(jax.random.fold_in(own_key, 6), position), (parts,), jnp.float32, least / len(pieces), largest / len(pieces))
        return jnp.repeat(jnp.exp(steps), extent[position] // parts).reshape((-1,) + (1,) * (len(extent) - position - 1))

    factor_of = one(*pieces[0])
    for cut in pieces[1:]:
        factor_of = factor_of * one(*cut)
    return factor_of


def gaussian(key, shape, deviation, bound, split=(), held_as=jnp.bfloat16):
    factor_of = level_of(key, shape, split, -0.22, 0.18) if split else 1.0
    values = jax.random.normal(key, shape, jnp.float32) * deviation * factor_of
    return jnp.minimum(jnp.maximum(values, -bound), bound).astype(held_as)


def setup_inputs(seed: int = 0) -> dict:
    key_of = jax.random.split(jax.random.key(seed), 7)
    basis_grad = gaussian(key_of[0], (FF, FF), FF ** -0.5, 0.046875, ((0, 8), (1, 4)))
    query = gaussian(key_of[1], (FF, D), 1.0, 6.0, ((0, 4), (1, 8)))
    basis_act = gaussian(key_of[2], (D, D), D ** -0.5, 0.09375, ((0, 8), (1, 4)))
    eig_vals = jnp.clip(jnp.exp(math.log(5.0) - 4.6051702 * jax.random.uniform(key_of[3], (FF, D), jnp.float32) ** level_of(key_of[3], (FF, D), ((0, 8), (1, 4)), -0.2, 0.2)), 0.05, 5.0)
    grad_out = gaussian(key_of[4], (TOKENS, FF), FF ** -0.5, 0.046875, ((0, 4), (1, 4)))
    act_in = gaussian(key_of[5], (TOKENS, D), D ** -0.5, 0.09375, ((0, 4), (1, 4)))
    return dict(basis_grad=basis_grad, query=query, basis_act=basis_act, eig_vals=eig_vals, grad_out=grad_out, act_in=act_in)


damping = 0.1


def reference(basis_grad, query, basis_act, eig_vals, grad_out, act_in):
    rows = FF // N_TENSOR
    summed = jnp.zeros((FF, D), jnp.float32)
    for group in range(N_TENSOR):
        part = jnp.dot(basis_grad[:, group * rows:(group + 1) * rows], query[group * rows:(group + 1) * rows], preferred_element_type=jnp.float32)
        part = lax.optimization_barrier(part.astype(jnp.bfloat16))
        summed = summed + part.astype(jnp.float32)
    rotated = jnp.dot(summed.astype(jnp.bfloat16), basis_act, preferred_element_type=jnp.float32)
    precond = (rotated / (eig_vals + damping)).astype(jnp.bfloat16)
    grad_rot = jnp.dot(grad_out, basis_grad.T, preferred_element_type=jnp.float32)
    act_rot = jnp.dot(act_in, basis_act, preferred_element_type=jnp.float32).astype(jnp.bfloat16)
    weighted = jnp.dot(act_rot, precond.T, preferred_element_type=jnp.float32)
    scores = jnp.sum(grad_rot * weighted, axis=1)
    return precond, scores
```

```python
import jax
import jax.numpy as jnp
from jax import lax
from jax.sharding import PartitionSpec as P

damping = 0.1
bf16 = jnp.bfloat16
f32 = jnp.float32


def swap(x, axis, size, bit):
    return lax.ppermute(x, axis, [(i, i ^ bit) for i in range(size)])


def low_bit(m):
    return (m & -m).bit_length() - 1


def fetch(x, bits):
    got = [x]
    for m in range(1, 1 << len(bits)):
        low = low_bit(m)
        got.append(swap(got[m ^ (1 << low)], *bits[low]))
    return got


def fetch_split(x, bits):
    cut = x.shape[0] * 3 // 8 // 16 * 16
    got = [[x]]
    for m in range(1, 1 << len(bits)):
        low, high = low_bit(m), m.bit_length() - 1
        a, b = got[m ^ (1 << low)], got[m ^ (1 << high)]
        if low in (0, high):
            ways = [(piece, low) for piece in a]
        else:
            ways = [(jnp.concatenate(a, axis=0)[:cut], low), (jnp.concatenate(b, axis=0)[cut:], high)]
        pieces = []
        for piece, bit in ways:
            pieces.append(swap(piece, *bits[bit]))
        got.append(pieces)
    return got


def line_sum(part, size):
    total = part.astype(f32)
    last = None
    for h in range(1, size):
        send = part if last is None else (part.astype(f32) + last.astype(f32)).astype(bf16)
        last = lax.ppermute(send, "tensor", [(h - 1, h), (size - h, size - h - 1)])
        total = total + last.astype(f32)
    return total


def make_body(n_tensor, n_dp, n_section):
    def bits_of(axis, size):
        return [(axis, size, 1 << b) for b in range(size.bit_length() - 1)]

    section_bits = bits_of("section", n_section)
    plane_bits = section_bits + bits_of("dp", n_dp)
    n_plane = n_section * n_dp

    def body(basis_grad, query, basis_act, eig_vals, grad_out, act_in):
        return steps(basis_grad, query, basis_act, eig_vals, grad_out, act_in)

    def steps(basis_grad, query, basis_act, eig_vals, grad_out, act_in):
        t = lax.axis_index("tensor")
        s = lax.axis_index("section")
        r = lax.axis_index("dp") * n_section + s
        rows = basis_grad.shape[0]
        depth, cols = basis_act.shape
        share = cols // n_plane
        wide = act_in.shape[1]

        def all_tokens(x):
            got = fetch(x, section_bits)
            whole = jnp.zeros((x.shape[0] * n_section, x.shape[1]), x.dtype)
            for m, piece in enumerate(got):
                whole = lax.dynamic_update_slice(whole, piece, ((s ^ m) * x.shape[0], 0))
            return whole

        own = []
        for m in range(n_plane):
            part = lax.dynamic_slice_in_dim(basis_act, (r ^ m) * share, share, 1)
            if m:
                part = lax.ppermute(part, ("dp", "section"), [(i, i ^ m) for i in range(n_plane)])
            own.append(part)
        mine = jnp.concatenate(own, axis=0)
        basis = lax.all_gather(mine, "tensor", axis=1, tiled=True)
        act_tokens = all_tokens(act_in)
        grad_tokens = all_tokens(grad_out)
        queries = fetch_split(query, plane_bits)

        pieces = []
        for g in range(2):
            n = grad_tokens.shape[0] // 2
            part = jnp.einsum(
                "ti,ei->te", grad_tokens[g * n : (g + 1) * n], basis_grad, preferred_element_type=f32
            ).astype(bf16)
            pieces.append(line_sum(part, n_tensor).astype(bf16))
        grad_rot = jnp.concatenate(pieces, axis=0)

        act_part = 0.0
        for i in range(wide // depth):
            slot = (t * (wide // depth) + i) ^ r
            some = lax.dynamic_slice_in_dim(basis, slot * depth, depth, 0)
            act_part = act_part + jnp.dot(act_tokens[:, i * depth : (i + 1) * depth], some, preferred_element_type=f32)
        act_part = act_part.astype(bf16)
        basis, act_part = lax.optimization_barrier((basis, act_part))
        act_rot = lax.psum_scatter(act_part, "tensor", scatter_dimension=1, tiled=True)
        acts = fetch(act_rot, plane_bits)

        late = (n_plane - 2) * depth
        whole = [jnp.concatenate(pieces, axis=0) for pieces in queries[: n_plane - 2]]
        turned = jnp.dot(jnp.concatenate(whole, axis=1), basis[:late], preferred_element_type=f32)
        turns = []
        start = 0
        for pair in zip(*queries[n_plane - 2 :]):
            stop = start + pair[0].shape[0]
            term = jnp.dot(jnp.concatenate(pair, axis=1), basis[late:], preferred_element_type=f32)
            turns.append((turned[start:stop] + term).astype(bf16))
            start = stop
        turned = jnp.concatenate(turns, axis=0)
        turns = fetch(turned, plane_bits)

        precond = jnp.zeros((rows, cols), bf16)
        value = 0.0
        groups = [[0], [1]] + [[m, m + 1] for m in range(2, n_plane, 2)]
        for group in groups:
            parts = []
            for m in group:
                parts.append(jnp.dot(basis_grad, turns[m], preferred_element_type=f32).astype(bf16))
            rotated = lax.psum_scatter(
                jnp.concatenate(parts, axis=0), "tensor", scatter_dimension=1, tiled=True
            )
            for i, m in enumerate(group):
                place = (r ^ m) * share
                eig = lax.dynamic_slice_in_dim(eig_vals, place, share, 1)
                piece = (rotated[i * rows : (i + 1) * rows].astype(f32) / (eig + damping)).astype(bf16)
                precond = lax.dynamic_update_slice(precond, piece, (0, place))
                folded = jnp.dot(grad_rot, piece, preferred_element_type=f32)
                value = value + jnp.sum(folded * acts[m].astype(f32), axis=1)

        for axis, size, bit in plane_bits + bits_of("tensor", n_tensor):
            value = value + swap(value, axis, size, bit)
        out = value.shape[0] // n_tensor
        return (precond, lax.dynamic_slice_in_dim(value, t * out, out, 0))

    return body


def solution(mesh):
    sizes = tuple(mesh.shape[name] for name in ("tensor", "dp", "section"))
    return jax.shard_map(
        make_body(*sizes),
        mesh=mesh,
        in_specs=(
            P(("dp", "section"), "tensor"),
            P("tensor", ("dp", "section")),
            P(("dp", "section"), "tensor"),
            P(("dp", "section"), "tensor"),
            P("section", "tensor"),
            P("section", "tensor"),
        ),
        out_specs=(P(("dp", "section"), "tensor"), P("tensor")),
        check_vma=False,
    )
```

```python
import functools
import math

import jax
import jax.numpy as jnp
from jax import lax
from jax.experimental import pallas as pl
from jax.sharding import PartitionSpec as P

damping = 0.1
bf16 = jnp.bfloat16
f32 = jnp.float32
plane = ("dp", "section")


def swap(x, axis, size, bit):
    return lax.ppermute(x, axis, [(i, i ^ bit) for i in range(size)])


def low_bit(m):
    return (m & -m).bit_length() - 1


def fetch(x, bits):
    got = [x]
    for m in range(1, 1 << len(bits)):
        low = low_bit(m)
        got.append(swap(got[m ^ (1 << low)], *bits[low]))
    return got


def fetch_split(x, bits, cut):
    got = [[x]]
    for m in range(1, 1 << len(bits)):
        low, high = low_bit(m), m.bit_length() - 1
        a, b = got[m ^ (1 << low)], got[m ^ (1 << high)]
        if m == 2:
            ways = [(x[:cut], low), (x[cut:], low)]
        elif low in (0, high):
            ways = [(piece, low) for piece in a]
        else:
            ways = [(a[0] if len(a) > 1 else a[0][:cut], low), (b[1] if len(b) > 1 else b[0][cut:], high)]
        pieces = []
        for piece, bit in ways:
            pieces.append(swap(piece, *bits[bit]))
        got.append(pieces)
    return got


def line_sum(part, size):
    total = part.astype(f32)
    last = None
    for h in range(1, size):
        send = part if last is None else (part.astype(f32) + last.astype(f32)).astype(bf16)
        last = lax.ppermute(send, "tensor", [(h - 1, h), (size - h, size - h - 1)])
        total = total + last.astype(f32)
    return total


def cost(flops, arrays):
    size = sum(math.prod(x.shape) * x.dtype.itemsize for x in arrays)
    return pl.CostEstimate(flops=flops, bytes_accessed=size, transcendentals=0)


def turn_kernel(depth, cut, counts, *refs):
    refs = list(refs)
    out, basis = refs.pop(), refs.pop()
    blocks = [[refs.pop() for _ in range(count)][::-1] for count in reversed(counts)][::-1]
    at = pl.program_id(0)

    def run(side):
        value = refs[0][...] if refs else None
        for m, pieces in enumerate(blocks):
            term = jnp.dot(
                pieces[min(side, len(pieces) - 1)][...],
                basis[m * depth : (m + 1) * depth],
                preferred_element_type=f32,
            )
            value = term if value is None else value + term
        out[...] = value.astype(out.dtype)

    @pl.when(at < cut)
    def _():
        run(0)

    @pl.when(at >= cut)
    def _():
        run(1)


def turn(total, blocks, basis, cut, dtype):
    rows = sum(piece.shape[0] for piece in blocks[0])
    depth = blocks[0][0].shape[1]
    cols = basis.shape[1]
    step = math.gcd(cut, rows)
    n = cut // step
    part = depth * len(blocks)
    place = 0 if total is None else basis.shape[0] // part - 1
    whole = pl.BlockSpec((step, depth), lambda i: (i, 0))
    first = pl.BlockSpec((step, depth), lambda i: (jnp.minimum(i, n - 1), 0))
    second = pl.BlockSpec((step, depth), lambda i: (jnp.maximum(i - n, 0), 0))
    tile = pl.BlockSpec((step, cols), lambda i: (i, 0))
    specs = [] if total is None else [tile]
    flat = [] if total is None else [total]
    for pieces in blocks:
        specs += [whole] if len(pieces) == 1 else [first, second]
        flat += pieces
    out = jax.ShapeDtypeStruct((rows, cols), dtype)
    return pl.pallas_call(
        functools.partial(turn_kernel, depth, n, [len(pieces) for pieces in blocks]),
        grid=(rows // step,),
        in_specs=specs + [pl.BlockSpec((part, cols), lambda i: (place, 0))],
        out_specs=tile,
        out_shape=out,
        cost_estimate=cost(2 * rows * part * cols, [*flat, out]),
    )(*flat, basis)


def pair_kernel(left, *refs):
    *rights, out = refs
    share = out.shape[-1]
    for i, right in enumerate(rights):
        value = jnp.dot(left[...], right[...], preferred_element_type=f32).astype(out.dtype)
        for z in range(out.shape[0]):
            out[z, i] = value[:, z * share : (z + 1) * share]


def pair_dot(left, rights, groups, step):
    rows, depth = left.shape
    cols = rights[0].shape[1]
    out = jax.ShapeDtypeStruct((groups, len(rights), rows, cols // groups), bf16)
    return pl.pallas_call(
        pair_kernel,
        grid=(rows // step,),
        in_specs=[pl.BlockSpec((step, depth), lambda i: (i, 0))]
        + [pl.BlockSpec((depth, cols), lambda i: (0, 0))] * len(rights),
        out_specs=pl.BlockSpec((groups, len(rights), step, cols // groups), lambda i: (0, 0, i, 0)),
        out_shape=out,
        cost_estimate=cost(2 * rows * depth * cols * len(rights), [left, *rights, out]),
    )(left, *rights)


def make_body(n_tensor, n_dp, n_section):
    def bits_of(axis, size):
        return [(axis, size, 1 << b) for b in range(size.bit_length() - 1)]

    section_bits = bits_of("section", n_section)
    plane_bits = section_bits + bits_of("dp", n_dp)
    n_plane = n_section * n_dp
    n_early = n_plane - 2

    def steps(basis_grad, query, basis_act, eig_vals, grad_out, act_in):
        t = lax.axis_index("tensor")
        s = lax.axis_index("section")
        r = lax.axis_index("dp") * n_section + s
        rows, units = basis_grad.shape
        depth, cols = basis_act.shape
        share = cols // n_plane
        wide = act_in.shape[1]
        cut = units * 3 // 8 // 16 * 16

        def all_tokens(x):
            got = fetch(x, section_bits)
            whole = jnp.zeros((x.shape[0] * n_section, x.shape[1]), x.dtype)
            for m, piece in enumerate(got):
                whole = lax.dynamic_update_slice(whole, piece, ((s ^ m) * x.shape[0], 0))
            return whole

        own = []
        for m in range(n_plane):
            part = lax.dynamic_slice_in_dim(basis_act, (r ^ m) * share, share, 1)
            if m:
                part = lax.ppermute(part, plane, [(i, i ^ m) for i in range(n_plane)])
            own.append(part)
        mine = jnp.concatenate(own, axis=0)
        basis = lax.all_gather(mine, "tensor", axis=1, tiled=True)
        act_tokens = all_tokens(act_in)
        grad_tokens = all_tokens(grad_out)
        queries = fetch_split(query, plane_bits, cut)

        pieces = []
        for g in range(2):
            n = grad_tokens.shape[0] // 2
            part = jnp.einsum(
                "ti,ei->te", grad_tokens[g * n : (g + 1) * n], basis_grad, preferred_element_type=f32
            ).astype(bf16)
            pieces.append(line_sum(part, n_tensor).astype(bf16))
        grad_rot = jnp.concatenate(pieces, axis=0)

        act_part = 0.0
        for i in range(wide // depth):
            slot = (t * (wide // depth) + i) ^ r
            some = lax.dynamic_slice_in_dim(basis, slot * depth, depth, 0)
            act_part = act_part + jnp.dot(
                act_tokens[:, i * depth : (i + 1) * depth], some, preferred_element_type=f32
            )
        act_rot = lax.psum_scatter(act_part.astype(bf16), "tensor", scatter_dimension=1, tiled=True)
        acts = fetch(act_rot, plane_bits)

        turned = turn(None, queries[:n_early], basis, cut, f32)
        turned = turn(turned, queries[n_early:], basis, cut, bf16)
        turns = fetch(turned, plane_bits)

        precond = jnp.zeros((rows, cols), bf16)
        value = 0.0
        for m in range(0, n_plane, 2):
            parts = pair_dot(basis_grad, turns[m : m + 2], n_tensor, math.gcd(rows, 256))
            parts = parts.reshape(n_tensor, 2 * rows, share)
            rotated = lax.psum_scatter(parts, "tensor", scatter_dimension=0, tiled=False)
            for i in range(2):
                place = (r ^ (m + i)) * share
                eig = lax.dynamic_slice_in_dim(eig_vals, place, share, 1)
                piece = (rotated[i * rows : (i + 1) * rows].astype(f32) / (eig + damping)).astype(bf16)
                precond = lax.dynamic_update_slice(precond, piece, (0, place))
                folded = jnp.dot(grad_rot, piece, preferred_element_type=f32)
                value = value + jnp.sum(folded * acts[m + i].astype(f32), axis=1)

        for axis, size, bit in plane_bits + bits_of("tensor", n_tensor):
            value = value + swap(value, axis, size, bit)
        out = value.shape[0] // n_tensor
        return (precond, lax.dynamic_slice_in_dim(value, t * out, out, 0))

    return steps


def solution(mesh):
    sizes = tuple(mesh.shape[name] for name in ("tensor", "dp", "section"))
    weight = P(plane, "tensor")
    tokens = P("section", "tensor")
    return jax.shard_map(
        make_body(*sizes),
        mesh=mesh,
        in_specs=(weight, P("tensor", plane), weight, weight, tokens, tokens),
        out_specs=(weight, P("tensor")),
        check_vma=False,
    )
```

```python
import functools
import math

import jax
import jax.numpy as jnp
from jax import lax
from jax.experimental import pallas as pl
from jax.sharding import PartitionSpec as P

damping = 0.1
bf16 = jnp.bfloat16
f32 = jnp.float32
plane = ("dp", "section")


def swap(x, axis, size, bit):
    return lax.ppermute(x, axis, [(i, i ^ bit) for i in range(size)])


def low_bit(m):
    return (m & -m).bit_length() - 1


def fetch(x, bits):
    got = [x]
    for m in range(1, 1 << len(bits)):
        low = low_bit(m)
        got.append(swap(got[m ^ (1 << low)], *bits[low]))
    return got


def fetch_split(x, bits, cut):
    got = [[x]]
    for m in range(1, 1 << len(bits)):
        low, high = low_bit(m), m.bit_length() - 1
        a, b = got[m ^ (1 << low)], got[m ^ (1 << high)]
        if m == 2:
            ways = [(x[:cut], low), (x[cut:], low)]
        elif low in (0, high):
            ways = [(piece, low) for piece in a]
        else:
            ways = [(a[0] if len(a) > 1 else a[0][:cut], low), (b[1] if len(b) > 1 else b[0][cut:], high)]
        pieces = []
        for piece, bit in ways:
            pieces.append(swap(piece, *bits[bit]))
        got.append(pieces)
    return got


def fetch_halves(halves, bits):
    got = [list(halves)]
    for m in range(1, 1 << len(bits)):
        low, high = low_bit(m), m.bit_length() - 1
        pieces = []
        for i in range(2):
            bit = high if i and low else low
            pieces.append(swap(got[m ^ (1 << bit)][i], *bits[bit]))
        got.append(pieces)
    return got


def line_sum(part, size):
    total = part.astype(f32)
    last = None
    for h in range(1, size):
        send = part if last is None else (part.astype(f32) + last.astype(f32)).astype(bf16)
        last = lax.ppermute(send, "tensor", [(h - 1, h), (size - h, size - h - 1)])
        total = total + last.astype(f32)
    return total


def cost(flops, arrays):
    size = sum(math.prod(x.shape) * x.dtype.itemsize for x in arrays)
    return pl.CostEstimate(flops=flops, bytes_accessed=size, transcendentals=0)


def turn_kernel(depth, cut, counts, outs, *refs):
    refs = list(refs)
    outs = [refs.pop() for _ in range(outs)][::-1]
    basis = refs.pop()
    blocks = [[refs.pop() for _ in range(count)][::-1] for count in reversed(counts)][::-1]
    at = pl.program_id(0)

    def run(side):
        value = refs[0][...] if refs else None
        for m, pieces in enumerate(blocks):
            term = jnp.dot(
                pieces[min(side, len(pieces) - 1)][...],
                basis[m * depth : (m + 1) * depth],
                preferred_element_type=f32,
            )
            value = term if value is None else value + term
        return value.astype(outs[0].dtype)

    half = pl.num_programs(0) // len(outs)
    for side in range(2):
        for i, out in enumerate(outs):
            here = (at < cut) if side == 0 else (at >= cut)

            @pl.when(here & (at >= i * half) & (at < (i + 1) * half))
            def _(side=side, out=out):
                out[...] = run(side)


def turn(total, blocks, basis, cut, dtype, outs):
    rows = sum(piece.shape[0] for piece in blocks[0])
    depth = blocks[0][0].shape[1]
    cols = basis.shape[1]
    step = math.gcd(cut, rows)
    n = cut // step
    part = depth * len(blocks)
    place = 0 if total is None else basis.shape[0] // part - 1
    whole = pl.BlockSpec((step, depth), lambda i: (i, 0))
    first = pl.BlockSpec((step, depth), lambda i: (jnp.minimum(i, n - 1), 0))
    second = pl.BlockSpec((step, depth), lambda i: (jnp.maximum(i - n, 0), 0))
    tile = pl.BlockSpec((step, cols), lambda i: (i, 0))
    specs = [] if total is None else [tile]
    flat = [] if total is None else [total]
    for pieces in blocks:
        specs += [whole] if len(pieces) == 1 else [first, second]
        flat += pieces
    half = rows // step // outs
    out = [jax.ShapeDtypeStruct((rows // outs, cols), dtype)] * outs
    return pl.pallas_call(
        functools.partial(turn_kernel, depth, n, [len(pieces) for pieces in blocks], outs),
        grid=(rows // step,),
        in_specs=specs + [pl.BlockSpec((part, cols), lambda i: (place, 0))],
        out_specs=[
            pl.BlockSpec((step, cols), lambda i, k=k: (jnp.clip(i - k * half, 0, half - 1), 0)) for k in range(outs)
        ],
        out_shape=out,
        cost_estimate=cost(2 * rows * part * cols, [*flat, *out]),
    )(*flat, basis)


def parts_kernel(use, n_into, n_total, *refs):
    refs = list(refs)
    out = refs.pop()
    refs = refs[n_into:]
    total = refs.pop(0) if n_total else None
    left, *rights = refs
    half = left.shape[1] // 2
    for i in range(len(rights) // len(use)):
        value = total[i] if n_total else None
        for k, side in enumerate(use):
            term = jnp.dot(
                left[:, side * half : (side + 1) * half], rights[i * len(use) + k][...], preferred_element_type=f32
            )
            value = term if value is None else value + term
        if out.dtype == f32:
            out[i] = value
        else:
            share = out.shape[-1]
            value = value.astype(out.dtype)
            for z in range(out.shape[0]):
                out[z, i] = value[:, z * share : (z + 1) * share]


def parts_dot(left, rights, groups, use=(0, 1), total=None, final=True, into=None, slot=0, slots=1):
    rows, depth = left.shape
    step = math.gcd(rows, 256)
    count = len(rights)
    cols = rights[0][0].shape[1]
    flat = [right[side] for right in rights for side in use]
    plain = pl.BlockSpec((count, step, cols), lambda i: (0, i, 0))
    specs, args, alias = [], [], {}
    if into is not None:
        specs.append(pl.BlockSpec(memory_space=pl.ANY))
        args.append(into)
        alias = {0: 0}
    if total is not None:
        specs.append(plain)
        args.append(total)
    specs.append(pl.BlockSpec((step, depth), lambda i: (i, 0)))
    specs += [pl.BlockSpec((depth // 2, cols), lambda i: (0, 0))] * len(flat)
    if final:
        out = jax.ShapeDtypeStruct((groups, slots * count, rows, cols // groups), bf16)
        out_spec = pl.BlockSpec((groups, count, step, cols // groups), lambda i: (0, slot, i, 0))
    else:
        out = jax.ShapeDtypeStruct((count, rows, cols), f32)
        out_spec = plain
    return pl.pallas_call(
        functools.partial(parts_kernel, use, len(alias), total is not None),
        grid=(rows // step,),
        in_specs=specs,
        out_specs=out_spec,
        out_shape=out,
        input_output_aliases=alias,
        cost_estimate=cost(rows * depth * cols * len(flat), [left, *flat, out]),
    )(*args, left, *flat)


def make_body(n_tensor, n_dp, n_section):
    def bits_of(axis, size):
        return [(axis, size, 1 << b) for b in range(size.bit_length() - 1)]

    section_bits = bits_of("section", n_section)
    plane_bits = section_bits + bits_of("dp", n_dp)
    n_plane = n_section * n_dp
    n_early = n_plane - 2

    def steps(basis_grad, query, basis_act, eig_vals, grad_out, act_in):
        t = lax.axis_index("tensor")
        s = lax.axis_index("section")
        r = lax.axis_index("dp") * n_section + s
        rows, units = basis_grad.shape
        depth, cols = basis_act.shape
        share = cols // n_plane
        wide = act_in.shape[1]
        cut = units * 3 // 8 // 16 * 16

        def all_tokens(x):
            got = fetch(x, section_bits)
            whole = jnp.zeros((x.shape[0] * n_section, x.shape[1]), x.dtype)
            for m, piece in enumerate(got):
                whole = lax.dynamic_update_slice(whole, piece, ((s ^ m) * x.shape[0], 0))
            return whole

        own = []
        for m in range(n_plane):
            part = lax.dynamic_slice_in_dim(basis_act, (r ^ m) * share, share, 1)
            if m:
                part = lax.ppermute(part, plane, [(i, i ^ m) for i in range(n_plane)])
            own.append(part)
        mine = jnp.concatenate(own, axis=0)
        basis = lax.all_gather(mine, "tensor", axis=1, tiled=True)
        act_tokens = all_tokens(act_in)
        grad_tokens = all_tokens(grad_out)
        queries = fetch_split(query, plane_bits, cut)

        pieces = []
        for g in range(2):
            n = grad_tokens.shape[0] // 2
            part = jnp.einsum(
                "ti,ei->te", grad_tokens[g * n : (g + 1) * n], basis_grad, preferred_element_type=f32
            ).astype(bf16)
            pieces.append(line_sum(part, n_tensor).astype(bf16))
        grad_rot = jnp.concatenate(pieces, axis=0)

        act_part = 0.0
        for i in range(wide // depth):
            slot = (t * (wide // depth) + i) ^ r
            some = lax.dynamic_slice_in_dim(basis, slot * depth, depth, 0)
            act_part = act_part + jnp.dot(act_tokens[:, i * depth : (i + 1) * depth], some, preferred_element_type=f32)
        act_rot = lax.psum_scatter(act_part.astype(bf16), "tensor", scatter_dimension=1, tiled=True)
        acts = fetch(act_rot, plane_bits)

        (turned,) = turn(None, queries[:n_early], basis, cut, f32, 1)
        turned = turn(turned, queries[n_early:], basis, cut, bf16, 2)
        turns = fetch_halves(turned, plane_bits)

        precond = jnp.zeros((rows, cols), bf16)
        value = 0.0
        groups = [[0, 1], [2, 3]] + [list(range(m, m + 4)) for m in range(4, n_plane, 4)]
        for group in groups:
            slots = len(group) // 2
            total = None
            if group[0] == 2:
                total = parts_dot(basis_grad, turns[2:4], n_tensor, (0,), final=False)
            parts = None
            for slot in range(slots):
                m = group[2 * slot]
                use = (0, 1) if total is None else (1,)
                parts = parts_dot(
                    basis_grad, turns[m : m + 2], n_tensor, use, total, into=parts, slot=slot, slots=slots
                )
            parts = parts.reshape(n_tensor, len(group) * rows, share)
            rotated = lax.psum_scatter(parts, "tensor", scatter_dimension=0, tiled=False)
            pieces = []
            for i, m in enumerate(group):
                place = (r ^ m) * share
                eig = lax.dynamic_slice_in_dim(eig_vals, place, share, 1)
                piece = (rotated[i * rows : (i + 1) * rows].astype(f32) / (eig + damping)).astype(bf16)
                folded = jnp.dot(grad_rot, piece, preferred_element_type=f32)
                value = value + jnp.sum(folded * acts[m].astype(f32), axis=1)
                pieces.append(piece)
            pieces, value, r = lax.optimization_barrier((pieces, value, r))
            for m, piece in zip(group, pieces):
                precond = lax.dynamic_update_slice(precond, piece, (0, (r ^ m) * share))

        for axis, size, bit in plane_bits + bits_of("tensor", n_tensor):
            value = value + swap(value, axis, size, bit)
        out = value.shape[0] // n_tensor
        return (precond, lax.dynamic_slice_in_dim(value, t * out, out, 0))

    return steps


def solution(mesh):
    sizes = tuple(mesh.shape[name] for name in ("tensor", "dp", "section"))
    weight = P(plane, "tensor")
    tokens = P("section", "tensor")
    return jax.shard_map(
        make_body(*sizes),
        mesh=mesh,
        in_specs=(weight, P("tensor", plane), weight, weight, tokens, tokens),
        out_specs=(weight, P("tensor")),
        check_vma=False,
    )
```
